256 devices in a mesh: member: 8 (over y, x_lo), space: 32 (over z, x_hi, core).
Axes of the slice: x: 4 (x_hi: 2, x_lo: 2; x = x_hi * 2 + x_lo), y: 4, z: 8, core: 2. Of those that a mesh axis runs over, the one named last changes fastest.
Arguments:
- concentration: float32 [64, 2, 8, 256, 1024], P('member', None, None, 'space'), may hold values from 0 to 2
- lhs_rows: int32 [64], P('member'), may hold values from 0 to 63
- source_table: float32 [64, 2, 8], replicated, may hold values from 0.05 to 0.5
- wind: bfloat16 [8, 2, 8, 256, 1024], P('member', None, None, 'space'), may hold values from -2 to 2
- diffusivity: bfloat16 [8, 8, 256, 1024], P('member', None, 'space'), may hold values from 0.019897461 to 0.119628906
- footprint: bfloat16 [256, 1024], P('space'), may hold values from 0.099609375 to 1
- settle: float32 [2, 8], replicated, may hold values from 0.05 to 0.4
- owner: int32 [8], replicated, may hold values from 0 to 7
Outputs:
- concentration_next: float32 [64, 2, 8, 256, 1024], P('member', None, None, 'space')
- deposition: float32 [64, 2, 256, 1024], P('member', None, 'space')
The draws below stay inside these ranges and needn't reach their ends.
All inputs are finite; a program needn't handle non-finite values.
Results may differ from the reference program's by a relative error of at most 0.0003.
Values may be sent and summed in bfloat16 or wider, within the bound.
A program may use at most 128 MiB of HBM per device.

```python
import math
import jax
import jax.numpy as jnp
from jax import lax

BINS = 2
LEV = 8
NY = 1024
ROWS = 64
MEMBERS = 64
SLABS = 8
NX = 256


def plant(array, key, smallest, largest):
    place = [jax.random.randint(jax.random.fold_in(key, axis), (), 0, length) for axis, length in enumerate(array.shape)]
    widest = array.shape.index(max(array.shape))
    neighbour = place[:widest] + [(place[widest] + 1) % array.shape[widest]] + place[widest + 1:]
    return array.at[tuple(place)].set(smallest).at[tuple(neighbour)].set(largest)


def shard_levels(key, extent, cuts, smallest, top_value):
    def one(position, parts):
        heights = jax.random.uniform(jax.random.fold_in(jax.random.fold_in(key, 6), position), (parts,), jnp.float32, smallest / len(cuts), top_value / len(cuts))
        return jnp.repeat(jnp.exp(heights), extent[position] // parts).reshape((-1,) + (1,) * (len(extent) - position - 1))

    level = one(*cuts[0])
    for cut in cuts[1:]:
        level = level * one(*cut)
    return level


def centred(key, extent, scale, most, cuts=(), held_as=jnp.bfloat16):
    gain = shard_levels(key, extent, cuts, -0.22, 0.18) if cuts else 1.0
    result = jax.random.normal(key, extent, jnp.float32) * scale * gain
    return jnp.minimum(jnp.maximum(result, -most), most).astype(held_as)


def setup_inputs(seed: int = 0) -> dict:
    seeds = jax.random.split(jax.random.key(seed), 9)
    return {
        "concentration": jnp.clip(2.0 * jax.random.uniform(seeds[0], (MEMBERS, BINS, LEV, NX, NY), jnp.float32) ** shard_levels(seeds[0], (MEMBERS, BINS, LEV, NX, NY), ((0, 8), (3, 32)), -0.2, 0.2), 0.0, 2.0),
        "lhs_rows": plant(jax.random.randint(seeds[1], (MEMBERS,), 0, ROWS), jax.random.fold_in(seeds[1], 1), 0, ROWS - 1).astype(jnp.int32),
        "source_table": jnp.clip(jnp.exp(jax.random.uniform(seeds[2], (ROWS, BINS, LEV), jnp.float32, math.log(0.05), math.log(0.5))), 0.05, 0.5),
        "wind": centred(seeds[3], (SLABS, 2, LEV, NX, NY), 0.15, 2.0, ((0, 8), (3, 32))),
        "diffusivity": jnp.clip(0.019897461 + 0.099731445 * jax.random.uniform(seeds[4], (SLABS, LEV, NX, NY), jnp.float32) ** shard_levels(seeds[4], (SLABS, LEV, NX, NY), ((0, 8), (2, 32)), -0.2, 0.2), 0.019897461, 0.119628906).astype(jnp.bfloat16),
        "footprint": jnp.clip(jnp.exp(math.log(1.0) - 2.306499 * jax.random.uniform(seeds[5], (NX, NY), jnp.float32) ** shard_levels(seeds[5], (NX, NY), ((0, 32),), -0.2, 0.2)), 0.099609375, 1.0).astype(jnp.bfloat16),
        "settle": jnp.clip(jnp.exp(jax.random.uniform(seeds[6], (BINS, LEV), jnp.float32, math.log(0.05), math.log(0.4))), 0.05, 0.4),
        "owner": plant(jax.random.randint(seeds[7], (LEV,), 0, SLABS), jax.random.fold_in(seeds[7], 1), 0, SLABS - 1).astype(jnp.int32),
    }


def tendency(cpad, metpad, settle, amp, levels):
    u = metpad[0:levels]
    v = metpad[levels:2 * levels]
    k = metpad[2 * levels:3 * levels]
    f = metpad[3 * levels]
    uf = 0.5 * (u[:, :-1] + u[:, 1:])
    kx = 0.5 * (k[:, :-1] + k[:, 1:])
    flux = jnp.maximum(uf, 0.0) * cpad[..., :-1, :] + jnp.minimum(uf, 0.0) * cpad[..., 1:, :] - kx * (cpad[..., 1:, :] - cpad[..., :-1, :])
    tend = -(flux[..., 1:, :] - flux[..., :-1, :])
    inner = cpad[..., 1:-1, :]
    cy = jnp.pad(inner, ((0, 0), (0, 0), (0, 0), (0, 0), (1, 1)))
    vy = jnp.pad(v[:, 1:-1], ((0, 0), (0, 0), (1, 1)))
    ky = jnp.pad(k[:, 1:-1], ((0, 0), (0, 0), (1, 1)))
    vf = 0.5 * (vy[..., :-1] + vy[..., 1:])
    kf = 0.5 * (ky[..., :-1] + ky[..., 1:])
    flux_y = jnp.maximum(vf, 0.0) * cy[..., :-1] + jnp.minimum(vf, 0.0) * cy[..., 1:] - kf * (cy[..., 1:] - cy[..., :-1])
    tend = tend - (flux_y[..., 1:] - flux_y[..., :-1])
    loss = settle[None, :, :, None, None] * inner
    above = jnp.concatenate([loss[:, :, 1:], jnp.zeros_like(loss[:, :, :1])], axis=2)
    tend = tend - loss + above + amp[:, :, :, None, None] * f[1:-1][None, None, None]
    return tend, loss[:, :, 0]


def reference(concentration, lhs_rows, source_table, wind, diffusivity, footprint, settle, owner):
    wind_levels = []
    diff_levels = []
    for level in range(LEV):
        slab = lax.dynamic_index_in_dim(wind, owner[level], 0, keepdims=False)
        wind_levels.append(slab[:, level])
        dslab = lax.dynamic_index_in_dim(diffusivity, owner[level], 0, keepdims=False)
        diff_levels.append(dslab[level])
    wind_now = jnp.stack(wind_levels, axis=1)
    diff_now = jnp.stack(diff_levels, axis=0)
    met = jnp.concatenate([wind_now.reshape(2 * LEV, NX, NY), diff_now, footprint[None]], axis=0).astype(jnp.float32)
    metpad = jnp.pad(met, ((0, 0), (1, 1), (0, 0)))
    amp = source_table[lhs_rows]
    padx = ((0, 0), (0, 0), (0, 0), (1, 1), (0, 0))
    start = concentration
    t0, g0 = tendency(jnp.pad(start, padx), metpad, settle, amp, LEV)
    c1 = start + t0
    t1, g1 = tendency(jnp.pad(c1, padx), metpad, settle, amp, LEV)
    c2 = 0.75 * start + 0.25 * (c1 + t1)
    t2, g2 = tendency(jnp.pad(c2, padx), metpad, settle, amp, LEV)
    final = (1.0 / 3.0) * start + (2.0 / 3.0) * (c2 + t2)
    deposit = g0 / 6.0 + g1 / 6.0 + (2.0 / 3.0) * g2
    return final, deposit
```

```python
import functools

import jax
import jax.numpy as jnp
from jax import lax
from jax.experimental import pallas as pl
from jax.experimental.pallas import tpu as pltpu
from jax.sharding import PartitionSpec as P

MESH = pl.DeviceIdType.MESH
H = 3
SCALE = 32767.0


def shifted(c, by):
    return pltpu.roll(c, by % c.shape[1], 1)


def kernel(
    dims,
    conc, wind, diff, foot, lhs, table, settle, owner,
    out, dep,
    cbuf, c1, c2, obuf, ql, qr, ht, hb,
    own, cand0, cand1, pair0, pair1, mets, m32, mt, mhs, mhr, fbuf, fh, fB,
    aC, aE, aW, aN, aS, amp, sU,
    s_conc, s_met, s_foot, s_tr, s_out,
    p1s, p1r, p2s, p2r, ags, agr, mss, msr, fss, fsr, hss, hsr,
):
    M, B, L, R, C, NS = dims
    cand, pair = (cand0, cand1), (pair0, pair1)
    T = R + 2 * H
    me = lax.axis_index("member")
    sp = lax.axis_index("space")
    y = lax.div(me, 2)
    xl = lax.rem(me, 2)
    left = (me, lax.rem(sp + NS - 1, NS))
    right = (me, lax.rem(sp + 1, NS))
    partner = (y * 2 + 1 - xl, sp)
    ypeers = [(lax.rem(y + d, 4) * 2 + xl, sp) for d in (1, 2, 3)]

    met_in = [
        pltpu.make_async_copy(wind.at[0, 0], own.at[:, 0], s_met.at[0]),
        pltpu.make_async_copy(wind.at[0, 1], own.at[:, 1], s_met.at[1]),
        pltpu.make_async_copy(diff.at[0], own.at[:, 2], s_met.at[2]),
    ]
    for cp in met_in:
        cp.start()
    foot_in = pltpu.make_async_copy(foot, fbuf, s_foot)
    foot_in.start()

    def conc_start(m, carry):
        for x in range(R):
            pltpu.make_async_copy(conc.at[m, :, :, x, :], cbuf.at[m, H + x], s_conc.at[m]).start()
        return carry

    lax.fori_loop(0, M, conc_start, 0)

    bar = pltpu.get_barrier_semaphore()
    for p in ypeers + [partner, left, right]:
        pl.semaphore_signal(bar, inc=1, device_id=p, device_id_type=MESH)
    pl.semaphore_wait(bar, 6)

    for cp in met_in:
        cp.wait()

    def p1(d, h):
        yp = lax.rem(y + d, 4)
        return pltpu.make_async_remote_copy(
            own.at[2 * yp + h], cand[h].at[y], p1s.at[d - 1, h], p1r.at[d - 1, h],
            device_id=ypeers[d - 1], device_id_type=MESH)

    for h in range(2):
        for d in (2, 1, 3):
            p1(d, h).start()
    for h in range(2):
        cand[h][y] = own[2 * y + h]

    foot_in.wait()
    f_send = [
        pltpu.make_async_remote_copy(fbuf, fh.at[i], fss.at[i], fsr.at[i], device_id=p, device_id_type=MESH)
        for i, p in enumerate((right, left))
    ]
    for cp in f_send:
        cp.start()

    def coded(m, r):
        both = jnp.concatenate([cbuf[m, r, b] for b in range(B)], axis=0)
        return ((both * SCALE + 0.5).astype(jnp.int32) - int(SCALE)).astype(jnp.int16)

    def halo(m, i):
        return pltpu.make_async_remote_copy(
            (qr, ql)[i].at[m], (ht, hb)[i].at[m], hss.at[i, m], hsr.at[i, m],
            device_id=(right, left)[i], device_id_type=MESH)

    def send_halo(m, carry):
        pltpu.make_async_copy(cbuf.at[m, pl.ds(H, R)], cbuf.at[m, pl.ds(H, R)], s_conc.at[m]).wait()
        for j in range(H):
            ql[m, j] = coded(m, H + j)
            qr[m, j] = coded(m, R + j)
        halo(m, 0).start()
        halo(m, 1).start()
        return carry

    lax.fori_loop(0, M, send_halo, 0)

    level = lax.broadcasted_iota(jnp.int32, (L, 128), 0)
    for b in range(B):
        up = jnp.zeros((L, 128), jnp.float32)
        for l in range(L - 1):
            up = jnp.where(level == l, settle[b, l + 1], up)
        sU[b] = up

    def emission(m, carry):
        row = lhs[m]
        for b in range(B):
            a = jnp.zeros((L, 128), jnp.float32)
            for l in range(L):
                a = jnp.where(level == l, table[row, b, l], a)
            amp[m, b] = a
        return carry

    lax.fori_loop(0, M, emission, 0)

    def p2(h):
        return pltpu.make_async_remote_copy(
            pair[h].at[xl], pair[h].at[xl], p2s.at[h], p2r.at[h], device_id=partner, device_id_type=MESH)

    def ag(d, h):
        return pltpu.make_async_remote_copy(
            mets.at[2 * y + h], mets.at[2 * y + h], ags.at[d - 1, h], agr.at[d - 1, h],
            device_id=ypeers[d - 1], device_id_type=MESH)

    for h in range(2):
        for d in (1, 2, 3):
            p1(d, h).wait_recv()
        o = owner[2 * y + h]
        pair[h][xl] = cand[h][lax.div(o, 2)]
        p2(h).start()
    for h in range(2):
        p2(h).wait_recv()
        o = owner[2 * y + h]
        mets[2 * y + h] = pair[h][lax.rem(o, 2)]
        for d in (2, 1, 3):
            ag(d, h).start()
    for h in range(2):
        for d in (1, 2, 3):
            ag(d, h).wait_recv()

    for l in range(L):
        for c in range(3):
            m32[c, l] = mets[l, c].astype(jnp.float32)
    for c in range(3):
        for x in range(R):
            pltpu.make_async_copy(m32.at[c, :, x, :], mt.at[c, H + x], s_tr.at[c]).start()
    for c in range(3):
        pltpu.make_async_copy(m32.at[c], mt.at[c, pl.ds(H, R)], s_tr.at[c]).wait()

    def met_halo(i):
        return pltpu.make_async_remote_copy(
            mhs.at[i], mhr.at[i], mss.at[i], msr.at[i], device_id=(right, left)[i], device_id_type=MESH)

    for i, base in enumerate((R, H)):
        for c in range(3):
            for j in range(H):
                mhs[i, c, j] = mt[c, base + j].astype(jnp.bfloat16)
        met_halo(i).start()

    lane = lax.broadcasted_iota(jnp.int32, (L, C), 1)
    inside_left = jnp.where(sp == 0, 0.0, 1.0).astype(jnp.float32)
    inside_right = jnp.where(sp == NS - 1, 0.0, 1.0).astype(jnp.float32)

    def face(u, k, w, q):
        uf = 0.5 * (u + w)
        kf = 0.5 * (k + q)
        return kf + jnp.maximum(uf, 0.0), kf - jnp.minimum(uf, 0.0)

    def coefficients(r, mask=None):
        u, k = mt[0, r], mt[2, r]
        pE, mE = face(u, k, mt[0, r + 1], mt[2, r + 1])
        pW, mW = face(mt[0, r - 1], mt[2, r - 1], u, k)
        v = mt[1, r]
        lo = lambda a: jnp.where(lane == 0, 0.0, shifted(a, 1))
        hi = lambda a: jnp.where(lane == C - 1, 0.0, shifted(a, -1))
        pS, mS = face(lo(v), lo(k), v, k)
        pN, mN = face(v, k, hi(v), hi(k))
        pS0 = jnp.where(lane == 0, 0.0, pS)
        mN0 = jnp.where(lane == C - 1, 0.0, mN)
        centre = 1.0 - (pE + mW + pN + mS)
        scaled = (lambda a: a) if mask is None else (lambda a: a * mask)
        aE[r] = scaled(mE)
        aW[r] = scaled(pW)
        aN[r] = scaled(mN0)
        aS[r] = scaled(pS0)
        for b in range(B):
            s = jnp.zeros((L, 128), jnp.float32)
            for l in range(L):
                s = jnp.where(level == l, settle[b, l], s)
            aC[b, r] = scaled(centre - jnp.tile(s, (1, C // 128)))

    def step(src, m, r, b):
        c = src[m, r, b]
        t = aC[b, r] * c
        t += aE[r] * src[m, r + 1, b]
        t += aW[r] * src[m, r - 1, b]
        t += aN[r] * shifted(c, -1)
        t += aS[r] * shifted(c, 1)
        t += jnp.tile(sU[b], (1, C // 128)) * pltpu.roll(c, L - 1, 0)
        t += jnp.tile(amp[m, b], (1, C // 128)) * fB[r]
        return t

    def stage1(m, r):
        for b in range(B):
            c1[m, r, b] = step(cbuf, m, r, b)

    def stage2(m, r):
        for b in range(B):
            c2[m, r, b] = 0.75 * cbuf[m, r, b] + 0.25 * step(c1, m, r, b)

    def stage3(m, r):
        for b in range(B):
            obuf[m, r - H, b] = (1.0 / 3.0) * cbuf[m, r, b] + (2.0 / 3.0) * step(c2, m, r, b)
            g = cbuf[m, r, b, 0:1, :] + c1[m, r, b, 0:1, :] + 4.0 * c2[m, r, b, 0:1, :]
            dep[m, b, r - H:r - H + 1, :] = g * (settle[b, 0] / 6.0)

    fown = fbuf[...].astype(jnp.float32)
    for x in range(R):
        fB[H + x] = jnp.broadcast_to(fown[x:x + 1, :], (L, C))
    for r in range(H + 1, H + R - 1):
        coefficients(r)

    def inner(m, carry):
        for r in range(H + 1, H + R - 1):
            stage1(m, r)
        for r in range(H + 2, H + R - 2):
            stage2(m, r)
        for r in range(H + 3, H + R - 3):
            stage3(m, r)
        return carry

    lax.fori_loop(0, M, inner, 0)

    for i in range(2):
        f_send[i].wait_recv()
        met_halo(i).wait_recv()
    for i, (base, mask) in enumerate(((0, inside_left), (H + R, inside_right))):
        for c in range(3):
            for j in range(H):
                mt[c, base + j] = mhr[i, c, j].astype(jnp.float32) * mask
        f = fh[i].astype(jnp.float32) * mask
        for j in range(H):
            x = (R - H + j) if i == 0 else j
            fB[base + j] = jnp.broadcast_to(f[x:x + 1, :], (L, C))
    for r in (1, 2):
        coefficients(r, inside_left)
    for r in (H, H + R - 1):
        coefficients(r)
    for r in (H + R, H + R + 1):
        coefficients(r, inside_right)

    def outer(m, carry):
        for i, (base, mask) in enumerate(((0, inside_left), (H + R, inside_right))):
            halo(m, i).wait_recv()
            for j in range(H):
                both = ((ht, hb)[i][m, j].astype(jnp.int32).astype(jnp.float32) + SCALE) * (mask * (1.0 / SCALE))
                for b in range(B):
                    cbuf[m, base + j, b] = both[b * L:(b + 1) * L]
        for r in (1, 2, 3, 10, 11, 12):
            stage1(m, r)
        for r in (2, 3, 4, 9, 10, 11):
            stage2(m, r)
        for r in (3, 4, 5, 8, 9, 10):
            stage3(m, r)
        for x in range(R):
            pltpu.make_async_copy(obuf.at[m, x], out.at[m, :, :, x, :], s_out.at[m]).start()
        return carry

    lax.fori_loop(0, M, outer, 0)

    def finish(m, carry):
        pltpu.make_async_copy(obuf.at[m], obuf.at[m], s_out.at[m]).wait()
        halo(m, 0).wait_send()
        halo(m, 1).wait_send()
        return carry

    lax.fori_loop(0, M, finish, 0)
    for h in range(2):
        for d in (1, 2, 3):
            p1(d, h).wait_send()
            ag(d, h).wait_send()
        p2(h).wait_send()
    for i in range(2):
        f_send[i].wait_send()
        met_halo(i).wait_send()


def on_device(ns, concentration, lhs_rows, source_table, wind, diffusivity, footprint, settle, owner):
    M, B, L, R, C = concentration.shape
    T = R + 2 * H
    f32, bf16, i16 = jnp.float32, jnp.bfloat16, jnp.int16
    hbm = pl.BlockSpec(memory_space=pltpu.HBM)
    smem = pl.BlockSpec(memory_space=pltpu.SMEM)
    vmem = pl.BlockSpec(memory_space=pltpu.VMEM)
    V, D = pltpu.VMEM, pltpu.SemaphoreType.DMA
    return pl.pallas_call(
        functools.partial(kernel, (M, B, L, R, C, ns)),
        out_shape=(
            jax.ShapeDtypeStruct((M, B, L, R, C), f32),
            jax.ShapeDtypeStruct((M, B, R, C), f32),
        ),
        in_specs=[hbm, hbm, hbm, hbm, smem, smem, smem, smem],
        out_specs=(vmem, vmem),
        scratch_shapes=[
            V((M, T, B, L, C), f32), V((M, T, B, L, C), f32), V((M, T, B, L, C), f32), V((M, R, B, L, C), f32),
            V((M, H, B * L, C), i16), V((M, H, B * L, C), i16), V((M, H, B * L, C), i16), V((M, H, B * L, C), i16),
            V((L, 3, R, C), bf16), V((4, 3, R, C), bf16), V((4, 3, R, C), bf16), V((2, 3, R, C), bf16), V((2, 3, R, C), bf16), V((L, 3, R, C), bf16),
            V((3, L, R, C), f32), V((3, T, L, C), f32), V((2, 3, H, L, C), bf16), V((2, 3, H, L, C), bf16),
            V((R, C), bf16), V((2, R, C), bf16), V((T, L, C), f32),
            V((B, T, L, C), f32), V((T, L, C), f32), V((T, L, C), f32), V((T, L, C), f32), V((T, L, C), f32),
            V((M, B, L, 128), f32), V((B, L, 128), f32),
            D((M,)), D((3,)), D, D((3,)), D((M,)),
            D((3, 2)), D((3, 2)), D((2,)), D((2,)), D((3, 2)), D((3, 2)), D((2,)), D((2,)), D((2,)), D((2,)),
            D((2, M)), D((2, M)),
        ],
        compiler_params=pltpu.CompilerParams(
            collective_id=0, has_side_effects=True, vmem_limit_bytes=56 << 20),
        name="transport",
    )(concentration, wind, diffusivity, footprint, lhs_rows, source_table, settle, owner)


def solution(mesh):
    cells = P("member", None, None, "space", None)
    return jax.shard_map(
        functools.partial(on_device, mesh.shape["space"]),
        mesh=mesh,
        in_specs=(cells, P("member"), P(), cells, P("member", None, "space", None), P("space", None), P(), P()),
        out_specs=(cells, P("member", None, "space", None)),
        check_vma=False,
    )
```

```python
import functools

import jax
import jax.numpy as jnp
from jax import lax
from jax.experimental import pallas as pl
from jax.experimental.pallas import tpu as pltpu
from jax.sharding import PartitionSpec as P

MESH = pl.DeviceIdType.MESH
H = 3
SCALE = 32767.0
PACE = (2, 3, 5)


def shifted(c, by):
    return pltpu.roll(c, by % c.shape[1], 1)


def kernel(
    dims,
    conc, wind, diff, foot, lhs, table, settle, owner,
    out, dep_out,
    cbuf, c1, c2, obuf, dep, ql, qr, ht, hb,
    own, cand0, cand1, pair0, pair1, mets, m32, mt, mhs, mhr, fbuf, fh, fB,
    aC, aE, aW, aN, aS, amp, sU,
    s_conc, s_met, s_foot, s_tr, s_out, s_dep,
    p1s, p1r, p2s, p2r, ags, agr, mss, msr, fss, fsr, hss, hsr,
):
    M, B, L, R, C, NS = dims
    cand, pair = (cand0, cand1), (pair0, pair1)
    T = R + 2 * H
    me = lax.axis_index("member")
    sp = lax.axis_index("space")
    y = lax.div(me, 2)
    xl = lax.rem(me, 2)
    left = (me, lax.rem(sp + NS - 1, NS))
    right = (me, lax.rem(sp + 1, NS))
    partner = (y * 2 + 1 - xl, sp)
    ypeers = [(lax.rem(y + d, 4) * 2 + xl, sp) for d in (1, 2, 3)]

    met_in = [
        pltpu.make_async_copy(wind.at[0, 0], own.at[:, 0], s_met.at[0]),
        pltpu.make_async_copy(wind.at[0, 1], own.at[:, 1], s_met.at[1]),
        pltpu.make_async_copy(diff.at[0], own.at[:, 2], s_met.at[2]),
    ]
    for cp in met_in:
        cp.start()
    foot_in = pltpu.make_async_copy(foot, fbuf, s_foot)
    foot_in.start()

    def conc_start(m, carry):
        for x in range(R):
            pltpu.make_async_copy(conc.at[m, :, :, x, :], cbuf.at[m, H + x], s_conc.at[m]).start()
        return carry

    lax.fori_loop(0, M, conc_start, 0)

    bar = pltpu.get_barrier_semaphore()
    for p in ypeers + [partner, left, right]:
        pl.semaphore_signal(bar, inc=1, device_id=p, device_id_type=MESH)
    pl.semaphore_wait(bar, 6)

    for cp in met_in:
        cp.wait()

    def p1(d, h):
        yp = lax.rem(y + d, 4)
        return pltpu.make_async_remote_copy(
            own.at[2 * yp + h], cand[h].at[y], p1s.at[d - 1, h], p1r.at[d - 1, h],
            device_id=ypeers[d - 1], device_id_type=MESH)

    for h in range(2):
        for d in (2, 1, 3):
            p1(d, h).start()
    for h in range(2):
        cand[h][y] = own[2 * y + h]

    foot_in.wait()
    f_send = [
        pltpu.make_async_remote_copy(fbuf, fh.at[i], fss.at[i], fsr.at[i], device_id=p, device_id_type=MESH)
        for i, p in enumerate((right, left))
    ]
    for cp in f_send:
        cp.start()

    def coded(m, r):
        both = jnp.concatenate([cbuf[m, r, b] for b in range(B)], axis=0)
        return ((both * SCALE + 0.5).astype(jnp.int32) - int(SCALE)).astype(jnp.int16)

    def halo(m, i):
        return pltpu.make_async_remote_copy(
            (qr, ql)[i].at[m], (ht, hb)[i].at[m], hss.at[i, m], hsr.at[i, m],
            device_id=(right, left)[i], device_id_type=MESH)

    def send_halo(m, carry):
        pltpu.make_async_copy(cbuf.at[m, pl.ds(H, R)], cbuf.at[m, pl.ds(H, R)], s_conc.at[m]).wait()
        for j in range(H):
            ql[m, j] = coded(m, H + j)
            qr[m, j] = coded(m, R + j)
        halo(m, 0).start()
        halo(m, 1).start()
        return carry

    lax.fori_loop(0, PACE[0], send_halo, 0)

    level = lax.broadcasted_iota(jnp.int32, (L, 128), 0)
    for b in range(B):
        up = jnp.zeros((L, 128), jnp.float32)
        for l in range(L - 1):
            up = jnp.where(level == l, settle[b, l + 1], up)
        sU[b] = up

    def emission(m, carry):
        row = lhs[m]
        for b in range(B):
            a = jnp.zeros((L, 128), jnp.float32)
            for l in range(L):
                a = jnp.where(level == l, table[b, l, row], a)
            amp[m, b] = a
        return carry

    lax.fori_loop(0, M, emission, 0)

    def p2(h):
        return pltpu.make_async_remote_copy(
            pair[h].at[xl], pair[h].at[xl], p2s.at[h], p2r.at[h], device_id=partner, device_id_type=MESH)

    def ag(d, h):
        return pltpu.make_async_remote_copy(
            mets.at[2 * y + h], mets.at[2 * y + h], ags.at[d - 1, h], agr.at[d - 1, h],
            device_id=ypeers[d - 1], device_id_type=MESH)

    for h in range(2):
        for d in (1, 2, 3):
            p1(d, h).wait_recv()
        o = owner[2 * y + h]
        pair[h][xl] = cand[h][lax.div(o, 2)]
        p2(h).start()
    lax.fori_loop(PACE[0], PACE[1], send_halo, 0)
    for h in range(2):
        p2(h).wait_recv()
        o = owner[2 * y + h]
        mets[2 * y + h] = pair[h][lax.rem(o, 2)]
        for d in (2, 1, 3):
            ag(d, h).start()
    lax.fori_loop(PACE[1], PACE[2], send_halo, 0)
    for h in range(2):
        for d in (1, 2, 3):
            ag(d, h).wait_recv()

    for l in range(L):
        for c in range(3):
            m32[c, l] = mets[l, c].astype(jnp.float32)
    for c in range(3):
        for x in range(R):
            pltpu.make_async_copy(m32.at[c, :, x, :], mt.at[c, H + x], s_tr.at[c]).start()
    for c in range(3):
        pltpu.make_async_copy(m32.at[c], mt.at[c, pl.ds(H, R)], s_tr.at[c]).wait()

    def met_halo(i):
        return pltpu.make_async_remote_copy(
            mhs.at[i], mhr.at[i], mss.at[i], msr.at[i], device_id=(right, left)[i], device_id_type=MESH)

    for i, base in enumerate((R, H)):
        for c in range(3):
            for j in range(H):
                mhs[i, c, j] = mt[c, base + j].astype(jnp.bfloat16)
        met_halo(i).start()
    lax.fori_loop(PACE[2], M, send_halo, 0)

    lane = lax.broadcasted_iota(jnp.int32, (L, C), 1)
    inside_left = jnp.where(sp == 0, 0.0, 1.0).astype(jnp.float32)
    inside_right = jnp.where(sp == NS - 1, 0.0, 1.0).astype(jnp.float32)

    def face(u, k, w, q):
        uf = 0.5 * (u + w)
        kf = 0.5 * (k + q)
        return kf + jnp.maximum(uf, 0.0), kf - jnp.minimum(uf, 0.0)

    def coefficients(r, mask=None):
        u, k = mt[0, r], mt[2, r]
        pE, mE = face(u, k, mt[0, r + 1], mt[2, r + 1])
        pW, mW = face(mt[0, r - 1], mt[2, r - 1], u, k)
        v = mt[1, r]
        lo = lambda a: jnp.where(lane == 0, 0.0, shifted(a, 1))
        hi = lambda a: jnp.where(lane == C - 1, 0.0, shifted(a, -1))
        pS, mS = face(lo(v), lo(k), v, k)
        pN, mN = face(v, k, hi(v), hi(k))
        pS0 = jnp.where(lane == 0, 0.0, pS)
        mN0 = jnp.where(lane == C - 1, 0.0, mN)
        centre = 1.0 - (pE + mW + pN + mS)
        scaled = (lambda a: a) if mask is None else (lambda a: a * mask)
        aE[r] = scaled(mE)
        aW[r] = scaled(pW)
        aN[r] = scaled(mN0)
        aS[r] = scaled(pS0)
        for b in range(B):
            s = jnp.zeros((L, 128), jnp.float32)
            for l in range(L):
                s = jnp.where(level == l, settle[b, l], s)
            aC[b, r] = scaled(centre - jnp.tile(s, (1, C // 128)))

    def step(src, m, r, b):
        c = src[m, r, b]
        t = aC[b, r] * c
        t += aE[r] * src[m, r + 1, b]
        t += aW[r] * src[m, r - 1, b]
        t += aN[r] * shifted(c, -1)
        t += aS[r] * shifted(c, 1)
        t += jnp.tile(sU[b], (1, C // 128)) * pltpu.roll(c, L - 1, 0)
        t += jnp.tile(amp[m, b], (1, C // 128)) * fB[r]
        return t

    def stage1(m, r):
        for b in range(B):
            c1[m, r, b] = step(cbuf, m, r, b)

    def stage2(m, r):
        for b in range(B):
            c2[m, r, b] = 0.75 * cbuf[m, r, b] + 0.25 * step(c1, m, r, b)

    def stage3(m, r):
        for b in range(B):
            obuf[m, r - H, b] = (1.0 / 3.0) * cbuf[m, r, b] + (2.0 / 3.0) * step(c2, m, r, b)
            g = cbuf[m, r, b, 0:1, :] + c1[m, r, b, 0:1, :] + 4.0 * c2[m, r, b, 0:1, :]
            dep[m, b, r - H:r - H + 1, :] = g * (settle[b, 0] / 6.0)

    fown = fbuf[...].astype(jnp.float32)
    for x in range(R):
        fB[H + x] = jnp.broadcast_to(fown[x:x + 1, :], (L, C))
    for r in range(H + 1, H + R - 1):
        coefficients(r)

    def inner(m, carry):
        for r in range(H + 1, H + R - 1):
            stage1(m, r)
        for r in range(H + 2, H + R - 2):
            stage2(m, r)
        for r in range(H + 3, H + R - 3):
            stage3(m, r)
        return carry

    lax.fori_loop(0, M, inner, 0)

    for i in range(2):
        f_send[i].wait_recv()
        met_halo(i).wait_recv()
    for i, (base, mask) in enumerate(((0, inside_left), (H + R, inside_right))):
        for c in range(3):
            for j in range(H):
                mt[c, base + j] = mhr[i, c, j].astype(jnp.float32) * mask
        f = fh[i].astype(jnp.float32) * mask
        for j in range(H):
            x = (R - H + j) if i == 0 else j
            fB[base + j] = jnp.broadcast_to(f[x:x + 1, :], (L, C))
    for r in (1, 2):
        coefficients(r, inside_left)
    for r in (H, H + R - 1):
        coefficients(r)
    for r in (H + R, H + R + 1):
        coefficients(r, inside_right)

    def outer(m, carry):
        for i, (base, mask) in enumerate(((0, inside_left), (H + R, inside_right))):
            halo(m, i).wait_recv()
            for j in range(H):
                both = ((ht, hb)[i][m, j].astype(jnp.int32).astype(jnp.float32) + SCALE) * (mask * (1.0 / SCALE))
                for b in range(B):
                    cbuf[m, base + j, b] = both[b * L:(b + 1) * L]
        for r in (1, 2, 3, 10, 11, 12):
            stage1(m, r)
        for r in (2, 3, 4, 9, 10, 11):
            stage2(m, r)
        for r in (3, 4, 5, 8, 9, 10):
            stage3(m, r)
        for x in range(R):
            pltpu.make_async_copy(obuf.at[m, x], out.at[m, :, :, x, :], s_out.at[m]).start()
        pltpu.make_async_copy(dep.at[m], dep_out.at[m], s_dep.at[m]).start()
        return carry

    lax.fori_loop(0, M, outer, 0)

    def finish(m, carry):
        pltpu.make_async_copy(obuf.at[m], obuf.at[m], s_out.at[m]).wait()
        pltpu.make_async_copy(dep.at[m], dep_out.at[m], s_dep.at[m]).wait()
        halo(m, 0).wait_send()
        halo(m, 1).wait_send()
        return carry

    lax.fori_loop(0, M, finish, 0)
    for h in range(2):
        for d in (1, 2, 3):
            p1(d, h).wait_send()
            ag(d, h).wait_send()
        p2(h).wait_send()
    for i in range(2):
        f_send[i].wait_send()
        met_halo(i).wait_send()


def on_device(ns, concentration, lhs_rows, source_table, wind, diffusivity, footprint, settle, owner):
    M, B, L, R, C = concentration.shape
    T = R + 2 * H
    f32, bf16, i16 = jnp.float32, jnp.bfloat16, jnp.int16
    hbm = pl.BlockSpec(memory_space=pltpu.HBM)
    anym = pl.BlockSpec(memory_space=pl.ANY)
    smem = pl.BlockSpec(memory_space=pltpu.SMEM)
    vmem = pl.BlockSpec(memory_space=pltpu.VMEM)
    V, D = pltpu.VMEM, pltpu.SemaphoreType.DMA
    return pl.pallas_call(
        functools.partial(kernel, (M, B, L, R, C, ns)),
        out_shape=(
            jax.ShapeDtypeStruct((M, B, L, R, C), f32),
            jax.ShapeDtypeStruct((M, B, R, C), f32),
        ),
        in_specs=[hbm, hbm, hbm, hbm, smem, smem, smem, smem],
        out_specs=(hbm, hbm),
        scratch_shapes=[
            V((M, T, B, L, C), f32), V((M, T, B, L, C), f32), V((M, T, B, L, C), f32), V((M, R, B, L, C), f32), V((M, B, R, C), f32),
            V((M, H, B * L, C), i16), V((M, H, B * L, C), i16), V((M, H, B * L, C), i16), V((M, H, B * L, C), i16),
            V((L, 3, R, C), bf16), V((4, 3, R, C), bf16), V((4, 3, R, C), bf16), V((2, 3, R, C), bf16), V((2, 3, R, C), bf16), V((L, 3, R, C), bf16),
            V((3, L, R, C), f32), V((3, T, L, C), f32), V((2, 3, H, L, C), bf16), V((2, 3, H, L, C), bf16),
            V((R, C), bf16), V((2, R, C), bf16), V((T, L, C), f32),
            V((B, T, L, C), f32), V((T, L, C), f32), V((T, L, C), f32), V((T, L, C), f32), V((T, L, C), f32),
            V((M, B, L, 128), f32), V((B, L, 128), f32),
            D((M,)), D((3,)), D, D((3,)), D((M,)), D((M,)),
            D((3, 2)), D((3, 2)), D((2,)), D((2,)), D((3, 2)), D((3, 2)), D((2,)), D((2,)), D((2,)), D((2,)),
            D((2, M)), D((2, M)),
        ],
        compiler_params=pltpu.CompilerParams(
            collective_id=0, has_side_effects=True, vmem_limit_bytes=56 << 20),
        name="transport",
    )(concentration, wind, diffusivity, footprint, lhs_rows, source_table.transpose(1, 2, 0), settle, owner)


def solution(mesh):
    cells = P("member", None, None, "space", None)
    return jax.shard_map(
        functools.partial(on_device, mesh.shape["space"]),
        mesh=mesh,
        in_specs=(cells, P("member"), P(), cells, P("member", None, "space", None), P("space", None), P(), P()),
        out_specs=(cells, P("member", None, "space", None)),
        check_vma=False,
    )
```

```python
import functools

import jax
import jax.numpy as jnp
from jax import lax
from jax.experimental import pallas as pl
from jax.experimental.pallas import tpu as pltpu
from jax.sharding import PartitionSpec as P

MESH = pl.DeviceIdType.MESH
H = 3
SCALE = 32767.0
WEIGHTS = (1.0, 0.25, 2.0 / 3.0)
PACE = (2, 3, 5)


def shifted(c, by):
    return pltpu.roll(c, by % c.shape[1], 1)


def kernel(
    dims,
    conc, wind, diff, foot, lhs, table, settle, owner,
    out, dep_out,
    cbuf, c1, c2, obuf, dep, ql, qr, ht, hb,
    own, cand0, cand1, pair0, pair1, mets, m32, mt, hsend, mhr, mh32, fbuf, fh, fB,
    aC, aE, aW, aN, aS, amp, sU,
    s_conc, s_met, s_foot, s_tr, s_trh, s_out, s_dep,
    p1s, p1r, p2s, p2r, ags, agr, mss, msr, fss, fsr, hss, hsr,
):
    M, B, L, R, C, NS = dims
    cand, pair = (cand0, cand1), (pair0, pair1)
    half = (pl.ds(0, C // 2), pl.ds(C // 2, C // 2))
    T = R + 2 * H
    me = lax.axis_index("member")
    sp = lax.axis_index("space")
    y = lax.div(me, 2)
    xl = lax.rem(me, 2)
    left = (me, lax.rem(sp + NS - 1, NS))
    right = (me, lax.rem(sp + 1, NS))
    partner = (y * 2 + 1 - xl, sp)
    ypeers = [(lax.rem(y + d, 4) * 2 + xl, sp) for d in (1, 2, 3)]

    met_in = [
        pltpu.make_async_copy(wind.at[0, 0], own.at[:, 0], s_met.at[0]),
        pltpu.make_async_copy(wind.at[0, 1], own.at[:, 1], s_met.at[1]),
        pltpu.make_async_copy(diff.at[0], own.at[:, 2], s_met.at[2]),
    ]
    for cp in met_in:
        cp.start()
    foot_in = pltpu.make_async_copy(foot, fbuf, s_foot)
    foot_in.start()

    def conc_start(m, carry):
        for x in range(R):
            pltpu.make_async_copy(conc.at[m, :, :, x, :], cbuf.at[m, H + x], s_conc.at[m]).start()
        return carry

    lax.fori_loop(0, M, conc_start, 0)

    bar = pltpu.get_barrier_semaphore()
    for p in ypeers + [partner, left, right]:
        pl.semaphore_signal(bar, inc=1, device_id=p, device_id_type=MESH)
    pl.semaphore_wait(bar, 6)

    for cp in met_in:
        cp.wait()

    def p1(d, h):
        yp = lax.rem(y + d, 4)
        return pltpu.make_async_remote_copy(
            own.at[pl.ds(2 * yp, 2), :, :, half[h]], cand[h].at[y], p1s.at[d - 1, h], p1r.at[d - 1, h],
            device_id=ypeers[d - 1], device_id_type=MESH)

    for h in range(2):
        for d in (2, 1, 3):
            p1(d, h).start()
    for h in range(2):
        cand[h][y] = own[pl.ds(2 * y, 2), :, :, half[h]]

    foot_in.wait()
    f_send = [
        pltpu.make_async_remote_copy(fbuf, fh.at[i], fss.at[i], fsr.at[i], device_id=p, device_id_type=MESH)
        for i, p in enumerate((right, left))
    ]
    for cp in f_send:
        cp.start()

    def coded(m, r):
        both = jnp.concatenate([cbuf[m, r, b] for b in range(B)], axis=0)
        return ((both * SCALE + 0.5).astype(jnp.int32) - int(SCALE)).astype(jnp.int16)

    def halo(m, i):
        return pltpu.make_async_remote_copy(
            (qr, ql)[i].at[m], (ht, hb)[i].at[m], hss.at[i, m], hsr.at[i, m],
            device_id=(right, left)[i], device_id_type=MESH)

    def landed(m, carry):
        pltpu.make_async_copy(cbuf.at[m, pl.ds(H, R)], cbuf.at[m, pl.ds(H, R)], s_conc.at[m]).wait()
        return carry

    def send_halo(m, carry):
        for j in range(H):
            ql[m, j] = coded(m, H + j)
            qr[m, j] = coded(m, R + j)
        halo(m, 0).start()
        halo(m, 1).start()
        return carry

    lax.fori_loop(0, M, landed, 0)
    lax.fori_loop(0, PACE[0], send_halo, 0)

    level = lax.broadcasted_iota(jnp.int32, (L, 128), 0)
    for b in range(B):
        up = jnp.zeros((L, 128), jnp.float32)
        for l in range(L - 1):
            up = jnp.where(level == l, settle[b, l + 1], up)
        for i, w in enumerate(WEIGHTS):
            sU[i, b] = up * w

    def emission(m, carry):
        row = lhs[m]
        for b in range(B):
            a = jnp.zeros((L, 128), jnp.float32)
            for l in range(L):
                a = jnp.where(level == l, table[b, l, row], a)
            for i, w in enumerate(WEIGHTS):
                amp[i, m, b] = a * w
        return carry

    lax.fori_loop(0, M, emission, 0)

    def p2(h):
        return pltpu.make_async_remote_copy(
            pair[h].at[xl], pair[h].at[xl], p2s.at[h], p2r.at[h], device_id=partner, device_id_type=MESH)

    def ag(d, h):
        return pltpu.make_async_remote_copy(
            mets.at[pl.ds(2 * y, 2), :, :, half[h]], mets.at[pl.ds(2 * y, 2), :, :, half[h]], ags.at[d - 1, h], agr.at[d - 1, h],
            device_id=ypeers[d - 1], device_id_type=MESH)

    for h in range(2):
        for d in (1, 2, 3):
            p1(d, h).wait_recv()
        for j in range(2):
            pair[h][xl, j] = cand[h][lax.div(owner[2 * y + j], 2), j]
        p2(h).start()
    lax.fori_loop(PACE[0], PACE[1], send_halo, 0)
    sub = lax.broadcasted_iota(jnp.int32, (R, C // 2), 0)

    def edges(u, v, k, i):
        if i == 0:
            u, k = pltpu.roll(u, 3, 0), pltpu.roll(k, 6, 0)
        else:
            k, v = pltpu.roll(k, 3, 0), pltpu.roll(v, 6, 0)
        return jnp.where(sub < 3, u, jnp.where(sub < 6, k, v)).astype(jnp.bfloat16)

    def met_halo(i, d, h):
        there = (i, pl.ds(2 * lax.rem(y + 4 - d, 4), 2), slice(None), half[h])
        return pltpu.make_async_remote_copy(
            hsend.at[there], mhr.at[there], mss.at[i, 2 * d + h], msr.at[i, 2 * d + h],
            device_id=(right, left)[i], device_id_type=MESH)

    def pass_edges(d, h):
        for j in range(2):
            l = 2 * lax.rem(y + 4 - d, 4) + j
            u, v, k = (mets[l, c, :, half[h]].astype(jnp.float32) for c in range(3))
            for i in range(2):
                hsend[i, l, :, half[h]] = edges(u, v, k, i)
            for c, a in enumerate((u, v, k)):
                m32[c, l, :, half[h]] = a
        for i in range(2):
            met_halo(i, d, h).start()

    for h in range(2):
        p2(h).wait_recv()
        for j in range(2):
            mets[2 * y + j, :, :, half[h]] = pair[h][lax.rem(owner[2 * y + j], 2), j]
        for d in (2, 1, 3):
            ag(d, h).start()
        pass_edges(0, h)
    lax.fori_loop(PACE[1], PACE[2], send_halo, 0)

    def arrive(h):
        for d in (1, 3, 2):
            ag(d, h).wait_recv()
            pass_edges(d, h)
        for c in range(3):
            for x in range(R):
                pltpu.make_async_copy(
                    m32.at[c, :, x, half[h]], mt.at[c, H + x, :, half[h]], s_tr.at[c, h]).start()
        for c in range(3):
            pltpu.make_async_copy(
                m32.at[c, :, :, half[h]], mt.at[c, pl.ds(H, R), :, half[h]], s_tr.at[c, h]).wait()

    lane = lax.broadcasted_iota(jnp.int32, (L, C), 1)
    inside_left = jnp.where(sp == 0, 0.0, 1.0).astype(jnp.float32)
    inside_right = jnp.where(sp == NS - 1, 0.0, 1.0).astype(jnp.float32)

    def face(u, k, w, q):
        uf = 0.5 * (u + w)
        kf = 0.5 * (k + q)
        return kf + jnp.maximum(uf, 0.0), kf - jnp.minimum(uf, 0.0)

    def coefficients(r, mask=None, cols=C):
        at = slice(0, cols)
        u, k, v = mt[0, r, :, at], mt[2, r, :, at], mt[1, r, :, at]
        pE, mE = face(u, k, mt[0, r + 1, :, at], mt[2, r + 1, :, at])
        pW, mW = face(mt[0, r - 1, :, at], mt[2, r - 1, :, at], u, k)
        lanes = lane[:, at]
        lo = lambda a: jnp.where(lanes == 0, 0.0, shifted(a, 1))
        hi = lambda a: jnp.where(lanes == C - 1, 0.0, shifted(a, -1))
        pS, mS = face(lo(v), lo(k), v, k)
        pN, mN = face(v, k, hi(v), hi(k))
        pS0 = jnp.where(lanes == 0, 0.0, pS)
        mN0 = jnp.where(lanes == C - 1, 0.0, mN)
        centre = 1.0 - (pE + mW + pN + mS)
        scaled = (lambda a: a) if mask is None else (lambda a: a * mask)

        def keep(ref, to, a):
            for i, w in enumerate(WEIGHTS):
                ref[(i,) + to + (slice(None), at)] = a if w == 1.0 else a * w

        keep(aE, (r,), scaled(mE))
        keep(aW, (r,), scaled(pW))
        keep(aN, (r,), scaled(mN0))
        keep(aS, (r,), scaled(pS0))
        for b in range(B):
            s = jnp.zeros((L, 128), jnp.float32)
            for l in range(L):
                s = jnp.where(level == l, settle[b, l], s)
            keep(aC, (b, r), scaled(centre - jnp.tile(s, (1, cols // 128))))

    def step(i, src, m, r, b, lo, hi):
        at, n, skip = slice(lo, hi), (hi - lo) // 128, 128 if lo else 0
        wide = src[m, r, b, :, lo - skip:hi]
        c = wide[:, skip:]
        t = aC[i, b, r, :, at] * c
        t += aE[i, r, :, at] * src[m, r + 1, b, :, at]
        t += aW[i, r, :, at] * src[m, r - 1, b, :, at]
        t += aN[i, r, :, at] * shifted(wide, -1)[:, skip:]
        t += aS[i, r, :, at] * shifted(wide, 1)[:, skip:]
        t += jnp.tile(sU[i, b], (1, n)) * pltpu.roll(c, L - 1, 0)
        t += jnp.tile(amp[i, m, b], (1, n)) * fB[r, :, at]
        return t

    def stage1(m, r, lo=0, hi=C):
        for b in range(B):
            c1[m, r, b, :, lo:hi] = step(0, cbuf, m, r, b, lo, hi)

    def stage2(m, r, lo=0, hi=C):
        for b in range(B):
            c2[m, r, b, :, lo:hi] = 0.75 * cbuf[m, r, b, :, lo:hi] + step(1, c1, m, r, b, lo, hi)

    def stage3(m, r, lo=0, hi=C):
        for b in range(B):
            obuf[m, r - H, b, :, lo:hi] = (1.0 / 3.0) * cbuf[m, r, b, :, lo:hi] + step(2, c2, m, r, b, lo, hi)

    def deposit(m):
        for b in range(B):
            rows = (m, pl.ds(H, R), b, 0)
            dep[m, b] = (cbuf[rows] + c1[rows] + 4.0 * c2[rows]) * (settle[b, 0] / 6.0)

    fown = fbuf[...].astype(jnp.float32)
    for x in range(R):
        fB[H + x] = jnp.broadcast_to(fown[x:x + 1, :], (L, C))

    def inner(lo, hi, m, carry):
        for r in range(H + 1, H + R - 1):
            stage1(m, r, lo, hi)
        for r in range(H + 2, H + R - 2):
            stage2(m, r, lo, hi)
        for r in range(H + 3, H + R - 3):
            stage3(m, r, lo, hi)
        return carry

    arrive(0)
    for r in range(H + 1, H + R - 1):
        coefficients(r, cols=C // 2)
    lax.fori_loop(0, M, functools.partial(inner, 0, C // 2), 0)
    arrive(1)
    lax.fori_loop(PACE[2], M, send_halo, 0)
    for r in range(H + 1, H + R - 1):
        coefficients(r)
    lax.fori_loop(0, M, functools.partial(inner, C // 2 - 128, C), 0)

    for i in range(2):
        f_send[i].wait_recv()
        for d in range(4):
            for h in range(2):
                met_halo(i, d, h).wait_recv()
    for i, (base, mask) in enumerate(((0, inside_left), (H + R, inside_right))):
        for l in range(L):
            mh32[i, l] = mhr[i, l].astype(jnp.float32) * mask
        places = [(0, base + j) for j in range(3)] + [(2, base + j) for j in range(3)] + [(1, base + 1 - i), (1, base + 2 - i)]
        for q, (c, row) in enumerate(places):
            pltpu.make_async_copy(mh32.at[i, :, q, :], mt.at[c, row], s_trh.at[i]).start()
        f = fh[i].astype(jnp.float32) * mask
        for j in range(H):
            x = (R - H + j) if i == 0 else j
            fB[base + j] = jnp.broadcast_to(f[x:x + 1, :], (L, C))
    for i in range(2):
        pltpu.make_async_copy(mh32.at[i], mh32.at[i], s_trh.at[i]).wait()
    for r in (1, 2):
        coefficients(r, inside_left)
    for r in (H, H + R - 1):
        coefficients(r)
    for r in (H + R, H + R + 1):
        coefficients(r, inside_right)

    def outer(m, carry):
        for i, (base, mask) in enumerate(((0, inside_left), (H + R, inside_right))):
            halo(m, i).wait_recv()
            for j in range(H):
                both = ((ht, hb)[i][m, j].astype(jnp.int32).astype(jnp.float32) + SCALE) * (mask * (1.0 / SCALE))
                for b in range(B):
                    cbuf[m, base + j, b] = both[b * L:(b + 1) * L]
        for r in (1, 2, 3, 10, 11, 12):
            stage1(m, r)
        for r in (2, 3, 4, 9, 10, 11):
            stage2(m, r)
        for r in (3, 4, 5, 8, 9, 10):
            stage3(m, r)
        deposit(m)
        for x in range(R):
            pltpu.make_async_copy(obuf.at[m, x], out.at[m, :, :, x, :], s_out.at[m]).start()
        pltpu.make_async_copy(dep.at[m], dep_out.at[m], s_dep.at[m]).start()
        return carry

    lax.fori_loop(0, M, outer, 0)

    def finish(m, carry):
        pltpu.make_async_copy(obuf.at[m], obuf.at[m], s_out.at[m]).wait()
        pltpu.make_async_copy(dep.at[m], dep_out.at[m], s_dep.at[m]).wait()
        halo(m, 0).wait_send()
        halo(m, 1).wait_send()
        return carry

    lax.fori_loop(0, M, finish, 0)
    for h in range(2):
        for d in (1, 2, 3):
            p1(d, h).wait_send()
            ag(d, h).wait_send()
        p2(h).wait_send()
    for i in range(2):
        f_send[i].wait_send()
        for d in range(4):
            for h in range(2):
                met_halo(i, d, h).wait_send()


def deliver(a, b, a_out, b_out, va, vb, sa, sb, ta, tb):
    M = a.shape[0]
    load = [pltpu.make_async_copy(a.at[m], va.at[m], sa.at[m]) for m in range(M)]
    load.append(pltpu.make_async_copy(b, vb, sb))
    store = [pltpu.make_async_copy(va.at[m], a_out.at[m], ta.at[m]) for m in range(M)]
    store.append(pltpu.make_async_copy(vb, b_out, tb))
    for cp in load:
        cp.start()
    for there, back in zip(load, store):
        there.wait()
        back.start()
    for cp in store:
        cp.wait()


def on_device(ns, concentration, lhs_rows, source_table, wind, diffusivity, footprint, settle, owner):
    M, B, L, R, C = concentration.shape
    T = R + 2 * H
    f32, bf16, i16 = jnp.float32, jnp.bfloat16, jnp.int16
    hbm = pl.BlockSpec(memory_space=pltpu.HBM)
    anym = pl.BlockSpec(memory_space=pl.ANY)
    smem = pl.BlockSpec(memory_space=pltpu.SMEM)
    vmem = pl.BlockSpec(memory_space=pltpu.VMEM)
    V, D = pltpu.VMEM, pltpu.SemaphoreType.DMA
    result = pl.pallas_call(
        functools.partial(kernel, (M, B, L, R, C, ns)),
        out_shape=(
            jax.ShapeDtypeStruct((M, B, L, R, C), f32),
            jax.ShapeDtypeStruct((M, B, R, C), f32),
        ),
        in_specs=[hbm, hbm, hbm, hbm, smem, smem, smem, smem],
        out_specs=(hbm, hbm),
        scratch_shapes=[
            V((M, T, B, L, C), f32), V((M, T, B, L, C), f32), V((M, T, B, L, C), f32), V((M, R, B, L, C), f32), V((M, B, R, C), f32),
            V((M, H, B * L, C), i16), V((M, H, B * L, C), i16), V((M, H, B * L, C), i16), V((M, H, B * L, C), i16),
            V((L, 3, R, C), bf16), V((4, 2, 3, R, C // 2), bf16), V((4, 2, 3, R, C // 2), bf16), V((2, 2, 3, R, C // 2), bf16), V((2, 2, 3, R, C // 2), bf16), V((L, 3, R, C), bf16),
            V((3, L, R, C), f32), V((3, T, L, C), f32), V((2, L, R, C), bf16), V((2, L, R, C), bf16), V((2, L, R, C), f32),
            V((R, C), bf16), V((2, R, C), bf16), V((T, L, C), f32),
            V((3, B, T, L, C), f32), V((3, T, L, C), f32), V((3, T, L, C), f32), V((3, T, L, C), f32), V((3, T, L, C), f32),
            V((3, M, B, L, 128), f32), V((3, B, L, 128), f32),
            D((M,)), D((3,)), D, D((3, 2)), D((2,)), D((M,)), D((M,)),
            D((3, 2)), D((3, 2)), D((2,)), D((2,)), D((3, 2)), D((3, 2)), D((2, L)), D((2, L)), D((2,)), D((2,)),
            D((2, M)), D((2, M)),
        ],
        compiler_params=pltpu.CompilerParams(
            collective_id=0, has_side_effects=True, vmem_limit_bytes=56 << 20),
        name="transport",
    )(concentration, wind, diffusivity, footprint, lhs_rows, source_table.transpose(1, 2, 0), settle, owner)
    return pl.pallas_call(
        deliver,
        out_shape=tuple(jax.ShapeDtypeStruct(r.shape, r.dtype) for r in result),
        in_specs=[hbm, hbm],
        out_specs=(hbm, hbm),
        scratch_shapes=[V(result[0].shape, f32), V(result[1].shape, f32), D((M,)), D, D((M,)), D],
        compiler_params=pltpu.CompilerParams(vmem_limit_bytes=56 << 20),
        name="deliver",
    )(*result)


def solution(mesh):
    cells = P("member", None, None, "space", None)
    return jax.shard_map(
        functools.partial(on_device, mesh.shape["space"]),
        mesh=mesh,
        in_specs=(cells, P("member"), P(), cells, P("member", None, "space", None), P("space", None), P(), P()),
        out_specs=(cells, P("member", None, "space", None)),
        check_vma=False,
    )
```

```python
import functools

import jax
import jax.numpy as jnp
from jax import lax
from jax.experimental import pallas as pl
from jax.experimental.pallas import tpu as pltpu
from jax.sharding import PartitionSpec as P

MESH = pl.DeviceIdType.MESH
H = 3
SCALE = 32767.0
WEIGHTS = (1.0, 0.25, 2.0 / 3.0)
PACE = (2, 3, 5)


def shifted(c, by):
    return pltpu.roll(c, by % c.shape[1], 1)


def kernel(
    dims,
    conc, wind, diff, foot, lhs, table, settle, owner,
    out, dep_out,
    cbuf, c1, c2, obuf, dep, ql, qr, ht, hb,
    own, cand0, cand1, pair0, pair1, mets, m32, mt, hsend, mhr, mh32, fbuf, fh, fB,
    aC, aE, aW, aN, aS, amp, sU,
    s_conc, s_met, s_foot, s_tr, s_trh, s_out, s_dep,
    p1s, p1r, p2s, p2r, ags, agr, mss, msr, fss, fsr, hss, hsr,
):
    M, B, L, R, C, NS = dims
    cand, pair = (cand0, cand1), (pair0, pair1)
    half = (pl.ds(0, C // 2), pl.ds(C // 2, C // 2))
    T = R + 2 * H
    me = lax.axis_index("member")
    sp = lax.axis_index("space")
    y = lax.div(me, 2)
    xl = lax.rem(me, 2)
    left = (me, lax.rem(sp + NS - 1, NS))
    right = (me, lax.rem(sp + 1, NS))
    partner = (y * 2 + 1 - xl, sp)
    ypeers = [(lax.rem(y + d, 4) * 2 + xl, sp) for d in (1, 2, 3)]

    met_in = [
        pltpu.make_async_copy(wind.at[0, 0], own.at[:, 0], s_met.at[0]),
        pltpu.make_async_copy(wind.at[0, 1], own.at[:, 1], s_met.at[1]),
        pltpu.make_async_copy(diff.at[0], own.at[:, 2], s_met.at[2]),
    ]
    for cp in met_in:
        cp.start()
    foot_in = pltpu.make_async_copy(foot, fbuf, s_foot)
    foot_in.start()

    def conc_start(m, carry):
        for x in range(R):
            pltpu.make_async_copy(conc.at[m, :, :, x, :], cbuf.at[m, H + x], s_conc.at[m]).start()
        return carry

    lax.fori_loop(0, M, conc_start, 0)

    bar = pltpu.get_barrier_semaphore()
    for p in ypeers + [partner, left, right]:
        pl.semaphore_signal(bar, inc=1, device_id=p, device_id_type=MESH)
    pl.semaphore_wait(bar, 6)

    for cp in met_in:
        cp.wait()

    def p1(d, h):
        yp = lax.rem(y + d, 4)
        return pltpu.make_async_remote_copy(
            own.at[pl.ds(2 * yp, 2), :, :, half[h]], cand[h].at[y], p1s.at[d - 1, h], p1r.at[d - 1, h],
            device_id=ypeers[d - 1], device_id_type=MESH)

    for h in range(2):
        for d in (2, 1, 3):
            p1(d, h).start()
    for h in range(2):
        cand[h][y] = own[pl.ds(2 * y, 2), :, :, half[h]]

    foot_in.wait()
    f_send = [
        pltpu.make_async_remote_copy(fbuf, fh.at[i], fss.at[i], fsr.at[i], device_id=p, device_id_type=MESH)
        for i, p in enumerate((right, left))
    ]
    for cp in f_send:
        cp.start()

    def coded(m, r):
        both = jnp.concatenate([cbuf[m, r, b] for b in range(B)], axis=0)
        return ((both * SCALE + 0.5).astype(jnp.int32) - int(SCALE)).astype(jnp.int16)

    def halo(m, i):
        return pltpu.make_async_remote_copy(
            (qr, ql)[i].at[m], (ht, hb)[i].at[m], hss.at[i, m], hsr.at[i, m],
            device_id=(right, left)[i], device_id_type=MESH)

    def landed(m, carry):
        pltpu.make_async_copy(cbuf.at[m, pl.ds(H, R)], cbuf.at[m, pl.ds(H, R)], s_conc.at[m]).wait()
        return carry

    def send_halo(m, carry):
        for j in range(H):
            ql[m, j] = coded(m, H + j)
            qr[m, j] = coded(m, R + j)
        halo(m, 0).start()
        halo(m, 1).start()
        return carry

    lax.fori_loop(0, M, landed, 0)
    lax.fori_loop(0, PACE[0], send_halo, 0)

    level = lax.broadcasted_iota(jnp.int32, (L, 128), 0)
    for b in range(B):
        up = jnp.zeros((L, 128), jnp.float32)
        for l in range(L - 1):
            up = jnp.where(level == l, settle[b, l + 1], up)
        for i, w in enumerate(WEIGHTS):
            sU[i, b] = up * w

    def emission(m, carry):
        row = lhs[m]
        for b in range(B):
            a = jnp.zeros((L, 128), jnp.float32)
            for l in range(L):
                a = jnp.where(level == l, table[b, l, row], a)
            for i, w in enumerate(WEIGHTS):
                amp[i, m, b] = a * w
        return carry

    lax.fori_loop(0, M, emission, 0)

    def p2(h):
        return pltpu.make_async_remote_copy(
            pair[h].at[xl], pair[h].at[xl], p2s.at[h], p2r.at[h], device_id=partner, device_id_type=MESH)

    def ag(d, h):
        return pltpu.make_async_remote_copy(
            mets.at[pl.ds(2 * y, 2), :, :, half[h]], mets.at[pl.ds(2 * y, 2), :, :, half[h]], ags.at[d - 1, h], agr.at[d - 1, h],
            device_id=ypeers[d - 1], device_id_type=MESH)

    for h in range(2):
        for d in (1, 2, 3):
            p1(d, h).wait_recv()
        for j in range(2):
            pair[h][xl, j] = cand[h][lax.div(owner[2 * y + j], 2), j]
        p2(h).start()
    lax.fori_loop(PACE[0], PACE[1], send_halo, 0)
    sub = lax.broadcasted_iota(jnp.int32, (R, C // 2), 0)

    def edges(u, v, k, i):
        if i == 0:
            u, k = pltpu.roll(u, 3, 0), pltpu.roll(k, 6, 0)
        else:
            k, v = pltpu.roll(k, 3, 0), pltpu.roll(v, 6, 0)
        return jnp.where(sub < 3, u, jnp.where(sub < 6, k, v)).astype(jnp.bfloat16)

    def met_halo(i, d, h):
        there = (i, pl.ds(2 * lax.rem(y + 4 - d, 4), 2), slice(None), half[h])
        return pltpu.make_async_remote_copy(
            hsend.at[there], mhr.at[there], mss.at[i, 2 * d + h], msr.at[i, 2 * d + h],
            device_id=(right, left)[i], device_id_type=MESH)

    def pass_edges(d, h):
        for j in range(2):
            l = 2 * lax.rem(y + 4 - d, 4) + j
            u, v, k = (mets[l, c, :, half[h]].astype(jnp.float32) for c in range(3))
            for i in range(2):
                hsend[i, l, :, half[h]] = edges(u, v, k, i)
            for c, a in enumerate((u, v, k)):
                m32[c, l, :, half[h]] = a
        for i in range(2):
            met_halo(i, d, h).start()

    for h in range(2):
        p2(h).wait_recv()
        for j in range(2):
            mets[2 * y + j, :, :, half[h]] = pair[h][lax.rem(owner[2 * y + j], 2), j]
        for d in (2, 1, 3):
            ag(d, h).start()
        pass_edges(0, h)
    lax.fori_loop(PACE[1], PACE[2], send_halo, 0)

    def arrive(h):
        for d in (1, 3, 2):
            ag(d, h).wait_recv()
            pass_edges(d, h)
        for c in range(3):
            for x in range(R):
                pltpu.make_async_copy(
                    m32.at[c, :, x, half[h]], mt.at[c, H + x, :, half[h]], s_tr.at[c, h]).start()
        for c in range(3):
            pltpu.make_async_copy(
                m32.at[c, :, :, half[h]], mt.at[c, pl.ds(H, R), :, half[h]], s_tr.at[c, h]).wait()

    lane = lax.broadcasted_iota(jnp.int32, (L, C), 1)
    inside_left = jnp.where(sp == 0, 0.0, 1.0).astype(jnp.float32)
    inside_right = jnp.where(sp == NS - 1, 0.0, 1.0).astype(jnp.float32)

    def face(u, k, w, q):
        uf = 0.5 * (u + w)
        kf = 0.5 * (k + q)
        return kf + jnp.maximum(uf, 0.0), kf - jnp.minimum(uf, 0.0)

    def coefficients(r, mask=None, cols=C):
        at = slice(0, cols)
        u, k, v = mt[0, r, :, at], mt[2, r, :, at], mt[1, r, :, at]
        pE, mE = face(u, k, mt[0, r + 1, :, at], mt[2, r + 1, :, at])
        pW, mW = face(mt[0, r - 1, :, at], mt[2, r - 1, :, at], u, k)
        lanes = lane[:, at]
        lo = lambda a: jnp.where(lanes == 0, 0.0, shifted(a, 1))
        hi = lambda a: jnp.where(lanes == C - 1, 0.0, shifted(a, -1))
        pS, mS = face(lo(v), lo(k), v, k)
        pN, mN = face(v, k, hi(v), hi(k))
        pS0 = jnp.where(lanes == 0, 0.0, pS)
        mN0 = jnp.where(lanes == C - 1, 0.0, mN)
        centre = 1.0 - (pE + mW + pN + mS)
        scaled = (lambda a: a) if mask is None else (lambda a: a * mask)

        def keep(ref, to, a):
            for i, w in enumerate(WEIGHTS):
                ref[(i,) + to + (slice(None), at)] = a if w == 1.0 else a * w

        keep(aE, (r,), scaled(mE))
        keep(aW, (r,), scaled(pW))
        keep(aN, (r,), scaled(mN0))
        keep(aS, (r,), scaled(pS0))
        for b in range(B):
            s = jnp.zeros((L, 128), jnp.float32)
            for l in range(L):
                s = jnp.where(level == l, settle[b, l], s)
            keep(aC, (b, r), scaled(centre - jnp.tile(s, (1, cols // 128))))

    def step(i, src, m, r, b, lo, hi):
        at, n, skip = slice(lo, hi), (hi - lo) // 128, 128 if lo else 0
        wide = src[m, r, b, :, lo - skip:hi]
        c = wide[:, skip:]
        t = aC[i, b, r, :, at] * c
        t += aE[i, r, :, at] * src[m, r + 1, b, :, at]
        t += aW[i, r, :, at] * src[m, r - 1, b, :, at]
        t += aN[i, r, :, at] * shifted(wide, -1)[:, skip:]
        t += aS[i, r, :, at] * shifted(wide, 1)[:, skip:]
        t += jnp.tile(sU[i, b], (1, n)) * pltpu.roll(c, L - 1, 0)
        t += jnp.tile(amp[i, m, b], (1, n)) * fB[r, :, at]
        return t

    def stage1(m, r, lo=0, hi=C):
        for b in range(B):
            c1[m, r, b, :, lo:hi] = step(0, cbuf, m, r, b, lo, hi)

    def stage2(m, r, lo=0, hi=C):
        for b in range(B):
            c2[m, r, b, :, lo:hi] = 0.75 * cbuf[m, r, b, :, lo:hi] + step(1, c1, m, r, b, lo, hi)

    def stage3(m, r, lo=0, hi=C):
        for b in range(B):
            obuf[m, r - H, b, :, lo:hi] = (1.0 / 3.0) * cbuf[m, r, b, :, lo:hi] + step(2, c2, m, r, b, lo, hi)

    def deposit(m):
        for b in range(B):
            rows = (m, pl.ds(H, R), b, 0)
            dep[m, b] = (cbuf[rows] + c1[rows] + 4.0 * c2[rows]) * (settle[b, 0] / 6.0)

    fown = fbuf[...].astype(jnp.float32)
    for x in range(R):
        fB[H + x] = jnp.broadcast_to(fown[x:x + 1, :], (L, C))

    def inner(lo, hi, m, carry):
        for r in range(H + 1, H + R - 1):
            stage1(m, r, lo, hi)
        for r in range(H + 2, H + R - 2):
            stage2(m, r, lo, hi)
        for r in range(H + 3, H + R - 3):
            stage3(m, r, lo, hi)
        return carry

    arrive(0)
    for r in range(H + 1, H + R - 1):
        coefficients(r, cols=C // 2)
    lax.fori_loop(0, M, functools.partial(inner, 0, C // 2), 0, unroll=2)
    arrive(1)
    lax.fori_loop(PACE[2], M, send_halo, 0)
    for r in range(H + 1, H + R - 1):
        coefficients(r)
    lax.fori_loop(0, M, functools.partial(inner, C // 2 - 128, C), 0, unroll=2)

    for i in range(2):
        f_send[i].wait_recv()
        for d in range(4):
            for h in range(2):
                met_halo(i, d, h).wait_recv()
    for i, (base, mask) in enumerate(((0, inside_left), (H + R, inside_right))):
        for l in range(L):
            mh32[i, l] = mhr[i, l].astype(jnp.float32) * mask
        places = [(0, base + j) for j in range(3)] + [(2, base + j) for j in range(3)] + [(1, base + 1 - i), (1, base + 2 - i)]
        for q, (c, row) in enumerate(places):
            pltpu.make_async_copy(mh32.at[i, :, q, :], mt.at[c, row], s_trh.at[i]).start()
        f = fh[i].astype(jnp.float32) * mask
        for j in range(H):
            x = (R - H + j) if i == 0 else j
            fB[base + j] = jnp.broadcast_to(f[x:x + 1, :], (L, C))
    for i in range(2):
        pltpu.make_async_copy(mh32.at[i], mh32.at[i], s_trh.at[i]).wait()
    for r in (1, 2):
        coefficients(r, inside_left)
    for r in (H, H + R - 1):
        coefficients(r)
    for r in (H + R, H + R + 1):
        coefficients(r, inside_right)

    def outer(pair_of, carry):
        members = (2 * pair_of, 2 * pair_of + 1)
        for m in members:
            for i in range(2):
                halo(m, i).wait_recv()
        for m in members:
            for i, (base, mask) in enumerate(((0, inside_left), (H + R, inside_right))):
                for j in range(H):
                    both = ((ht, hb)[i][m, j].astype(jnp.int32).astype(jnp.float32) + SCALE) * (mask * (1.0 / SCALE))
                    for b in range(B):
                        cbuf[m, base + j, b] = both[b * L:(b + 1) * L]
        for stage, rows in ((stage1, (1, 2, 3, 10, 11, 12)), (stage2, (2, 3, 4, 9, 10, 11)), (stage3, (3, 4, 5, 8, 9, 10))):
            for m in members:
                for r in rows:
                    stage(m, r)
        for m in members:
            deposit(m)
        for m in members:
            for x in range(R):
                pltpu.make_async_copy(obuf.at[m, x], out.at[m, :, :, x, :], s_out.at[m]).start()
            pltpu.make_async_copy(dep.at[m], dep_out.at[m], s_dep.at[m]).start()
        return carry

    lax.fori_loop(0, M // 2, outer, 0)

    def finish(m, carry):
        pltpu.make_async_copy(obuf.at[m], obuf.at[m], s_out.at[m]).wait()
        pltpu.make_async_copy(dep.at[m], dep_out.at[m], s_dep.at[m]).wait()
        halo(m, 0).wait_send()
        halo(m, 1).wait_send()
        return carry

    lax.fori_loop(0, M, finish, 0)
    for h in range(2):
        for d in (1, 2, 3):
            p1(d, h).wait_send()
            ag(d, h).wait_send()
        p2(h).wait_send()
    for i in range(2):
        f_send[i].wait_send()
        for d in range(4):
            for h in range(2):
                met_halo(i, d, h).wait_send()


def deliver(a, b, a_out, b_out, va, vb, sa, sb, ta, tb):
    M = a.shape[0]
    parts = [pl.ds(m, 2) for m in range(0, M, 2)]
    load = [pltpu.make_async_copy(a.at[p], va.at[p], sa.at[i]) for i, p in enumerate(parts)]
    load.append(pltpu.make_async_copy(b, vb, sb))
    store = [pltpu.make_async_copy(va.at[p], a_out.at[p], ta.at[i]) for i, p in enumerate(parts)]
    store.append(pltpu.make_async_copy(vb, b_out, tb))
    for cp in load:
        cp.start()
    for there, back in zip(load, store):
        there.wait()
        back.start()
    for cp in store:
        cp.wait()


def on_device(ns, concentration, lhs_rows, source_table, wind, diffusivity, footprint, settle, owner):
    M, B, L, R, C = concentration.shape
    T = R + 2 * H
    f32, bf16, i16 = jnp.float32, jnp.bfloat16, jnp.int16
    hbm = pl.BlockSpec(memory_space=pltpu.HBM)
    anym = pl.BlockSpec(memory_space=pl.ANY)
    smem = pl.BlockSpec(memory_space=pltpu.SMEM)
    vmem = pl.BlockSpec(memory_space=pltpu.VMEM)
    V, D = pltpu.VMEM, pltpu.SemaphoreType.DMA
    result = pl.pallas_call(
        functools.partial(kernel, (M, B, L, R, C, ns)),
        out_shape=(
            jax.ShapeDtypeStruct((M, B, L, R, C), f32),
            jax.ShapeDtypeStruct((M, B, R, C), f32),
        ),
        in_specs=[hbm, hbm, hbm, hbm, smem, smem, smem, smem],
        out_specs=(hbm, hbm),
        scratch_shapes=[
            V((M, T, B, L, C), f32), V((M, T, B, L, C), f32), V((M, T, B, L, C), f32), V((M, R, B, L, C), f32), V((M, B, R, C), f32),
            V((M, H, B * L, C), i16), V((M, H, B * L, C), i16), V((M, H, B * L, C), i16), V((M, H, B * L, C), i16),
            V((L, 3, R, C), bf16), V((4, 2, 3, R, C // 2), bf16), V((4, 2, 3, R, C // 2), bf16), V((2, 2, 3, R, C // 2), bf16), V((2, 2, 3, R, C // 2), bf16), V((L, 3, R, C), bf16),
            V((3, L, R, C), f32), V((3, T, L, C), f32), V((2, L, R, C), bf16), V((2, L, R, C), bf16), V((2, L, R, C), f32),
            V((R, C), bf16), V((2, R, C), bf16), V((T, L, C), f32),
            V((3, B, T, L, C), f32), V((3, T, L, C), f32), V((3, T, L, C), f32), V((3, T, L, C), f32), V((3, T, L, C), f32),
            V((3, M, B, L, 128), f32), V((3, B, L, 128), f32),
            D((M,)), D((3,)), D, D((3, 2)), D((2,)), D((M,)), D((M,)),
            D((3, 2)), D((3, 2)), D((2,)), D((2,)), D((3, 2)), D((3, 2)), D((2, L)), D((2, L)), D((2,)), D((2,)),
            D((2, M)), D((2, M)),
        ],
        compiler_params=pltpu.CompilerParams(
            collective_id=0, has_side_effects=True, vmem_limit_bytes=56 << 20),
        name="transport",
    )(concentration, wind, diffusivity, footprint, lhs_rows, source_table.transpose(1, 2, 0), settle, owner)
    return pl.pallas_call(
        deliver,
        out_shape=tuple(jax.ShapeDtypeStruct(r.shape, r.dtype) for r in result),
        in_specs=[hbm, hbm],
        out_specs=(hbm, hbm),
        scratch_shapes=[V(result[0].shape, f32), V(result[1].shape, f32), D((M,)), D, D((M,)), D],
        compiler_params=pltpu.CompilerParams(vmem_limit_bytes=56 << 20),
        name="deliver",
    )(*result)


def solution(mesh):
    cells = P("member", None, None, "space", None)
    return jax.shard_map(
        functools.partial(on_device, mesh.shape["space"]),
        mesh=mesh,
        in_specs=(cells, P("member"), P(), cells, P("member", None, "space", None), P("space", None), P(), P()),
        out_specs=(cells, P("member", None, "space", None)),
        check_vma=False,
    )
```

```python
import functools

import jax
import jax.numpy as jnp
from jax import lax
from jax.experimental import pallas as pl
from jax.experimental.pallas import tpu as pltpu
from jax.sharding import PartitionSpec as P

MESH = pl.DeviceIdType.MESH
H = 3
SCALE = 32767.0
WEIGHTS = (1.0, 0.25, 2.0 / 3.0)
PACE = (2, 3, 5)


def shifted(c, by):
    return pltpu.roll(c, by % c.shape[1], 1)


def kernel(
    dims,
    conc, wind, diff, foot, lhs, table, settle, owner,
    out, dep_out,
    cbuf, c1, c2, obuf, dep, ql, qr, ht, hb,
    own, cand0, cand1, pair0, pair1, mets, m32, mt, hsend, mhr, mh32, fbuf, fh, fB,
    aC, aE, aW, aN, aS, amp, sU,
    s_conc, s_met, s_foot, s_tr, s_trh, s_out, s_dep,
    p1s, p1r, p2s, p2r, ags, agr, mss, msr, fss, fsr, hss, hsr,
):
    M, B, L, R, C, NS = dims
    cand, pair = (cand0, cand1), (pair0, pair1)
    half = (pl.ds(0, C // 2), pl.ds(C // 2, C // 2))
    T = R + 2 * H
    me = lax.axis_index("member")
    sp = lax.axis_index("space")
    y = lax.div(me, 2)
    xl = lax.rem(me, 2)
    left = (me, lax.rem(sp + NS - 1, NS))
    right = (me, lax.rem(sp + 1, NS))
    partner = (y * 2 + 1 - xl, sp)
    ypeers = [(lax.rem(y + d, 4) * 2 + xl, sp) for d in (1, 2, 3)]

    met_in = [
        pltpu.make_async_copy(wind.at[0, 0], own.at[:, 0], s_met.at[0]),
        pltpu.make_async_copy(wind.at[0, 1], own.at[:, 1], s_met.at[1]),
        pltpu.make_async_copy(diff.at[0], own.at[:, 2], s_met.at[2]),
    ]
    for cp in met_in:
        cp.start()
    foot_in = pltpu.make_async_copy(foot, fbuf, s_foot)
    foot_in.start()

    def conc_start(m, carry):
        for x in range(R):
            pltpu.make_async_copy(conc.at[m, :, :, x, :], cbuf.at[m, H + x], s_conc.at[m]).start()
        return carry

    lax.fori_loop(0, M, conc_start, 0)

    bar = pltpu.get_barrier_semaphore()
    for p in ypeers + [partner, left, right]:
        pl.semaphore_signal(bar, inc=1, device_id=p, device_id_type=MESH)
    pl.semaphore_wait(bar, 6)

    for cp in met_in:
        cp.wait()

    def p1(d, h):
        yp = lax.rem(y + d, 4)
        return pltpu.make_async_remote_copy(
            own.at[pl.ds(2 * yp, 2), :, :, half[h]], cand[h].at[y], p1s.at[d - 1, h], p1r.at[d - 1, h],
            device_id=ypeers[d - 1], device_id_type=MESH)

    for h in range(2):
        for d in (2, 1, 3):
            p1(d, h).start()
    for h in range(2):
        cand[h][y] = own[pl.ds(2 * y, 2), :, :, half[h]]

    foot_in.wait()
    f_send = [
        pltpu.make_async_remote_copy(fbuf, fh.at[i], fss.at[i], fsr.at[i], device_id=p, device_id_type=MESH)
        for i, p in enumerate((right, left))
    ]
    for cp in f_send:
        cp.start()

    def coded(m, r):
        both = jnp.concatenate([cbuf[m, r, b] for b in range(B)], axis=0)
        return ((both * SCALE + 0.5).astype(jnp.int32) - int(SCALE)).astype(jnp.int16)

    def halo(m, i):
        return pltpu.make_async_remote_copy(
            (qr, ql)[i].at[m], (ht, hb)[i].at[m], hss.at[i, m], hsr.at[i, m],
            device_id=(right, left)[i], device_id_type=MESH)

    def landed(m, carry):
        pltpu.make_async_copy(cbuf.at[m, pl.ds(H, R)], cbuf.at[m, pl.ds(H, R)], s_conc.at[m]).wait()
        return carry

    def send_halo(m, carry):
        for j in range(H):
            ql[m, j] = coded(m, H + j)
            qr[m, j] = coded(m, R + j)
        halo(m, 0).start()
        halo(m, 1).start()
        return carry

    lax.fori_loop(0, M, landed, 0)
    lax.fori_loop(0, PACE[0], send_halo, 0)

    level = lax.broadcasted_iota(jnp.int32, (L, 128), 0)
    for b in range(B):
        up = jnp.zeros((L, 128), jnp.float32)
        for l in range(L - 1):
            up = jnp.where(level == l, settle[b, l + 1], up)
        for i, w in enumerate(WEIGHTS):
            sU[i, b] = up * w

    def emission(m, carry):
        row = lhs[m]
        for b in range(B):
            a = jnp.zeros((L, 128), jnp.float32)
            for l in range(L):
                a = jnp.where(level == l, table[b, l, row], a)
            for i, w in enumerate(WEIGHTS):
                amp[i, m, b] = a * w
        return carry

    lax.fori_loop(0, M, emission, 0)

    def p2(h):
        return pltpu.make_async_remote_copy(
            pair[h].at[xl], pair[h].at[xl], p2s.at[h], p2r.at[h], device_id=partner, device_id_type=MESH)

    def ag(d, h):
        return pltpu.make_async_remote_copy(
            mets.at[pl.ds(2 * y, 2), :, :, half[h]], mets.at[pl.ds(2 * y, 2), :, :, half[h]], ags.at[d - 1, h], agr.at[d - 1, h],
            device_id=ypeers[d - 1], device_id_type=MESH)

    for h in range(2):
        for d in (1, 2, 3):
            p1(d, h).wait_recv()
        for j in range(2):
            pair[h][xl, j] = cand[h][lax.div(owner[2 * y + j], 2), j]
        p2(h).start()
    lax.fori_loop(PACE[0], PACE[1], send_halo, 0)
    sub = lax.broadcasted_iota(jnp.int32, (R, C // 2), 0)

    def edges(u, v, k, i):
        if i == 0:
            u, k = pltpu.roll(u, 3, 0), pltpu.roll(k, 6, 0)
        else:
            k, v = pltpu.roll(k, 3, 0), pltpu.roll(v, 6, 0)
        return jnp.where(sub < 3, u, jnp.where(sub < 6, k, v)).astype(jnp.bfloat16)

    def met_halo(i, d, h):
        there = (i, pl.ds(2 * lax.rem(y + 4 - d, 4), 2), slice(None), half[h])
        return pltpu.make_async_remote_copy(
            hsend.at[there], mhr.at[there], mss.at[i, 2 * d + h], msr.at[i, 2 * d + h],
            device_id=(right, left)[i], device_id_type=MESH)

    def pass_edges(d, h):
        for j in range(2):
            l = 2 * lax.rem(y + 4 - d, 4) + j
            u, v, k = (mets[l, c, :, half[h]].astype(jnp.float32) for c in range(3))
            for i in range(2):
                hsend[i, l, :, half[h]] = edges(u, v, k, i)
            for c, a in enumerate((u, v, k)):
                m32[c, l, :, half[h]] = a
        for i in range(2):
            met_halo(i, d, h).start()

    for h in range(2):
        p2(h).wait_recv()
        for j in range(2):
            mets[2 * y + j, :, :, half[h]] = pair[h][lax.rem(owner[2 * y + j], 2), j]
        for d in (2, 1, 3):
            ag(d, h).start()
        pass_edges(0, h)
    lax.fori_loop(PACE[1], PACE[2], send_halo, 0)

    def arrive(h):
        for d in (1, 3, 2):
            ag(d, h).wait_recv()
            pass_edges(d, h)
        for c in range(3):
            for x in range(R):
                pltpu.make_async_copy(
                    m32.at[c, :, x, half[h]], mt.at[c, H + x, :, half[h]], s_tr.at[c, h]).start()
        for c in range(3):
            pltpu.make_async_copy(
                m32.at[c, :, :, half[h]], mt.at[c, pl.ds(H, R), :, half[h]], s_tr.at[c, h]).wait()

    lane = lax.broadcasted_iota(jnp.int32, (L, C), 1)
    inside_left = jnp.where(sp == 0, 0.0, 1.0).astype(jnp.float32)
    inside_right = jnp.where(sp == NS - 1, 0.0, 1.0).astype(jnp.float32)

    def face(u, k, w, q):
        uf = 0.5 * (u + w)
        kf = 0.5 * (k + q)
        return kf + jnp.maximum(uf, 0.0), kf - jnp.minimum(uf, 0.0)

    def coefficients(r, mask=None, cols=C):
        at = slice(0, cols)
        u, k, v = mt[0, r, :, at], mt[2, r, :, at], mt[1, r, :, at]
        pE, mE = face(u, k, mt[0, r + 1, :, at], mt[2, r + 1, :, at])
        pW, mW = face(mt[0, r - 1, :, at], mt[2, r - 1, :, at], u, k)
        lanes = lane[:, at]
        lo = lambda a: jnp.where(lanes == 0, 0.0, shifted(a, 1))
        hi = lambda a: jnp.where(lanes == C - 1, 0.0, shifted(a, -1))
        pS, mS = face(lo(v), lo(k), v, k)
        pN, mN = face(v, k, hi(v), hi(k))
        pS0 = jnp.where(lanes == 0, 0.0, pS)
        mN0 = jnp.where(lanes == C - 1, 0.0, mN)
        centre = 1.0 - (pE + mW + pN + mS)
        scaled = (lambda a: a) if mask is None else (lambda a: a * mask)

        def keep(ref, to, a):
            for i, w in enumerate(WEIGHTS):
                ref[(i,) + to + (slice(None), at)] = a if w == 1.0 else a * w

        keep(aE, (r,), scaled(mE))
        keep(aW, (r,), scaled(pW))
        keep(aN, (r,), scaled(mN0))
        keep(aS, (r,), scaled(pS0))
        for b in range(B):
            s = jnp.zeros((L, 128), jnp.float32)
            for l in range(L):
                s = jnp.where(level == l, settle[b, l], s)
            keep(aC, (b, r), scaled(centre - jnp.tile(s, (1, cols // 128))))

    def step(i, src, m, r, b, lo, hi):
        at, n, skip = slice(lo, hi), (hi - lo) // 128, 128 if lo else 0
        wide = src[m, r, b, :, lo - skip:hi]
        c = wide[:, skip:]
        t = aC[i, b, r, :, at] * c
        t += aE[i, r, :, at] * src[m, r + 1, b, :, at]
        t += aW[i, r, :, at] * src[m, r - 1, b, :, at]
        t += aN[i, r, :, at] * shifted(wide, -1)[:, skip:]
        t += aS[i, r, :, at] * shifted(wide, 1)[:, skip:]
        t += jnp.tile(sU[i, b], (1, n)) * pltpu.roll(c, L - 1, 0)
        t += jnp.tile(amp[i, m, b], (1, n)) * fB[r, :, at]
        return t

    def stage1(m, r, lo=0, hi=C):
        for b in range(B):
            c1[m, r, b, :, lo:hi] = step(0, cbuf, m, r, b, lo, hi)

    def stage2(m, r, lo=0, hi=C):
        for b in range(B):
            c2[m, r, b, :, lo:hi] = 0.75 * cbuf[m, r, b, :, lo:hi] + step(1, c1, m, r, b, lo, hi)

    def stage3(m, r, lo=0, hi=C):
        for b in range(B):
            obuf[m, r - H, b, :, lo:hi] = (1.0 / 3.0) * cbuf[m, r, b, :, lo:hi] + step(2, c2, m, r, b, lo, hi)

    def deposit(m):
        for b in range(B):
            rows = (m, pl.ds(H, R), b, 0)
            dep[m, b] = (cbuf[rows] + c1[rows] + 4.0 * c2[rows]) * (settle[b, 0] / 6.0)

    fown = fbuf[...].astype(jnp.float32)
    for x in range(R):
        fB[H + x] = jnp.broadcast_to(fown[x:x + 1, :], (L, C))

    def inner(lo, hi, m, carry):
        for r in range(H + 1, H + R - 1):
            stage1(m, r, lo, hi)
        for r in range(H + 2, H + R - 2):
            stage2(m, r, lo, hi)
        for r in range(H + 3, H + R - 3):
            stage3(m, r, lo, hi)
        return carry

    arrive(0)
    for r in range(H + 1, H + R - 1):
        coefficients(r, cols=C // 2)
    lax.fori_loop(0, M, functools.partial(inner, 0, C // 2), 0, unroll=2)
    arrive(1)
    lax.fori_loop(PACE[2], M, send_halo, 0)
    for r in range(H + 1, H + R - 1):
        coefficients(r)
    lax.fori_loop(0, M, functools.partial(inner, C // 2 - 128, C), 0, unroll=2)

    for i in range(2):
        f_send[i].wait_recv()
        for d in range(4):
            for h in range(2):
                met_halo(i, d, h).wait_recv()
    for i, (base, mask) in enumerate(((0, inside_left), (H + R, inside_right))):
        for l in range(L):
            mh32[i, l] = mhr[i, l].astype(jnp.float32) * mask
        places = [(0, base + j) for j in range(3)] + [(2, base + j) for j in range(3)] + [(1, base + 1 - i), (1, base + 2 - i)]
        for q, (c, row) in enumerate(places):
            pltpu.make_async_copy(mh32.at[i, :, q, :], mt.at[c, row], s_trh.at[i]).start()
        f = fh[i].astype(jnp.float32) * mask
        for j in range(H):
            x = (R - H + j) if i == 0 else j
            fB[base + j] = jnp.broadcast_to(f[x:x + 1, :], (L, C))
    for i in range(2):
        pltpu.make_async_copy(mh32.at[i], mh32.at[i], s_trh.at[i]).wait()
    for r in (1, 2):
        coefficients(r, inside_left)
    for r in (H, H + R - 1):
        coefficients(r)
    for r in (H + R, H + R + 1):
        coefficients(r, inside_right)

    def outer(pair_of, carry):
        members = (2 * pair_of, 2 * pair_of + 1)
        for m in members:
            for i in range(2):
                halo(m, i).wait_recv()
        for m in members:
            for i, (base, mask) in enumerate(((0, inside_left), (H + R, inside_right))):
                for j in range(H):
                    both = ((ht, hb)[i][m, j].astype(jnp.int32).astype(jnp.float32) + SCALE) * (mask * (1.0 / SCALE))
                    for b in range(B):
                        cbuf[m, base + j, b] = both[b * L:(b + 1) * L]
        for stage, rows in ((stage1, (1, 2, 3, 10, 11, 12)), (stage2, (2, 3, 4, 9, 10, 11))):
            for m in members:
                for r in rows:
                    stage(m, r)
        for m in members:
            for r in (3, 4, 5, 8, 9, 10):
                stage3(m, r)
            deposit(m)
            for x in range(R):
                pltpu.make_async_copy(obuf.at[m, x], out.at[m, :, :, x, :], s_out.at[m]).start()
            pltpu.make_async_copy(dep.at[m], dep_out.at[m], s_dep.at[m]).start()
        return carry

    lax.fori_loop(0, M // 2, outer, 0)

    def finish(m, carry):
        pltpu.make_async_copy(obuf.at[m], obuf.at[m], s_out.at[m]).wait()
        pltpu.make_async_copy(dep.at[m], dep_out.at[m], s_dep.at[m]).wait()
        halo(m, 0).wait_send()
        halo(m, 1).wait_send()
        return carry

    lax.fori_loop(0, M, finish, 0)
    for h in range(2):
        for d in (1, 2, 3):
            p1(d, h).wait_send()
            ag(d, h).wait_send()
        p2(h).wait_send()
    for i in range(2):
        f_send[i].wait_send()
        for d in range(4):
            for h in range(2):
                met_halo(i, d, h).wait_send()


def deliver(a, b, a_out, b_out, va, vb, sa, sb, ta, tb):
    M = a.shape[0]
    parts = [pl.ds(m, 2) for m in range(0, M, 2)]
    load = [pltpu.make_async_copy(a.at[p], va.at[p], sa.at[i]) for i, p in enumerate(parts)]
    load.append(pltpu.make_async_copy(b, vb, sb))
    store = [pltpu.make_async_copy(va.at[p], a_out.at[p], ta.at[i]) for i, p in enumerate(parts)]
    store.append(pltpu.make_async_copy(vb, b_out, tb))
    for cp in load:
        cp.start()
    for there, back in zip(load, store):
        there.wait()
        back.start()
    for cp in store:
        cp.wait()


def on_device(ns, concentration, lhs_rows, source_table, wind, diffusivity, footprint, settle, owner):
    M, B, L, R, C = concentration.shape
    T = R + 2 * H
    f32, bf16, i16 = jnp.float32, jnp.bfloat16, jnp.int16
    hbm = pl.BlockSpec(memory_space=pltpu.HBM)
    anym = pl.BlockSpec(memory_space=pl.ANY)
    smem = pl.BlockSpec(memory_space=pltpu.SMEM)
    vmem = pl.BlockSpec(memory_space=pltpu.VMEM)
    V, D = pltpu.VMEM, pltpu.SemaphoreType.DMA
    result = pl.pallas_call(
        functools.partial(kernel, (M, B, L, R, C, ns)),
        out_shape=(
            jax.ShapeDtypeStruct((M, B, L, R, C), f32),
            jax.ShapeDtypeStruct((M, B, R, C), f32),
        ),
        in_specs=[hbm, hbm, hbm, hbm, smem, smem, smem, smem],
        out_specs=(hbm, hbm),
        scratch_shapes=[
            V((M, T, B, L, C), f32), V((M, T, B, L, C), f32), V((M, T, B, L, C), f32), V((M, R, B, L, C), f32), V((M, B, R, C), f32),
            V((M, H, B * L, C), i16), V((M, H, B * L, C), i16), V((M, H, B * L, C), i16), V((M, H, B * L, C), i16),
            V((L, 3, R, C), bf16), V((4, 2, 3, R, C // 2), bf16), V((4, 2, 3, R, C // 2), bf16), V((2, 2, 3, R, C // 2), bf16), V((2, 2, 3, R, C // 2), bf16), V((L, 3, R, C), bf16),
            V((3, L, R, C), f32), V((3, T, L, C), f32), V((2, L, R, C), bf16), V((2, L, R, C), bf16), V((2, L, R, C), f32),
            V((R, C), bf16), V((2, R, C), bf16), V((T, L, C), f32),
            V((3, B, T, L, C), f32), V((3, T, L, C), f32), V((3, T, L, C), f32), V((3, T, L, C), f32), V((3, T, L, C), f32),
            V((3, M, B, L, 128), f32), V((3, B, L, 128), f32),
            D((M,)), D((3,)), D, D((3, 2)), D((2,)), D((M,)), D((M,)),
            D((3, 2)), D((3, 2)), D((2,)), D((2,)), D((3, 2)), D((3, 2)), D((2, L)), D((2, L)), D((2,)), D((2,)),
            D((2, M)), D((2, M)),
        ],
        compiler_params=pltpu.CompilerParams(
            collective_id=0, has_side_effects=True, vmem_limit_bytes=56 << 20),
        name="transport",
    )(concentration, wind, diffusivity, footprint, lhs_rows, source_table.transpose(1, 2, 0), settle, owner)
    return pl.pallas_call(
        deliver,
        out_shape=tuple(jax.ShapeDtypeStruct(r.shape, r.dtype) for r in result),
        in_specs=[hbm, hbm],
        out_specs=(hbm, hbm),
        scratch_shapes=[V(result[0].shape, f32), V(result[1].shape, f32), D((M,)), D, D((M,)), D],
        compiler_params=pltpu.CompilerParams(vmem_limit_bytes=56 << 20),
        name="deliver",
    )(*result)


def solution(mesh):
    cells = P("member", None, None, "space", None)
    return jax.shard_map(
        functools.partial(on_device, mesh.shape["space"]),
        mesh=mesh,
        in_specs=(cells, P("member"), P(), cells, P("member", None, "space", None), P("space", None), P(), P()),
        out_specs=(cells, P("member", None, "space", None)),
        check_vma=False,
    )
```
